32 devices in a mesh: tm: 8 (over z, x), lev: 4 (over y, core).
Axes of the slice: x: 2, y: 2, z: 4, core: 2. Of those that a mesh axis runs over, the one named last changes fastest.
Arguments:
- fields: bfloat16 [4, 32, 9, 16384], P('lev', 'tm'), may hold values from -18 to 18
- lengths: int32 [8], P('tm'), may hold values from 1 to 4, 24 in all
- owners: int32 [9], replicated, may hold values from 0 to 7, as said below
- thickness: float32 [4], replicated, may hold values from 0.2 to 5
Outputs:
- daily_means: float32 [4, 16, 1, 16384], P('lev', 'tm')
- column_means: float32 [16, 1, 16384], P('tm', None, 'lev')
The draws below stay inside these ranges and needn't reach their ends.
Inputs may be any that keep to these rules, and one draw needn't show every extreme that they name: `lengths`: the entries sum to 24 and the largest is exactly 4. `owners`: no index owns more than 2 tiles; some index owns exactly 2.
All inputs are finite; a program needn't handle non-finite values. No bound on the sum of `lengths` on one device may be relied on, other than what follows from the above.
Results may differ from the reference program's by a relative error of at most 0.0003.
Values may be sent and summed in bfloat16 or wider, within the bound.
No kernel may reach another device: no remote copies, remote signals or barrier semaphores. Data moves between devices by JAX's collectives and lax.ppermute only.
A program may use at most 128 MiB of HBM per device.

```python
import math
import jax
import jax.numpy as jnp
import numpy as np
from jax import lax

CELLS = 16384
MAXT = 2
CAP = 4
TILES = 9
STEPS = 24
DAYS = 1
LEVELS = 4
N_TM = 8


def draw_owners(key, part):
    shuffled = jax.random.permutation(key, MAXT * N_TM)
    return (shuffled[:TILES] % N_TM).astype(jnp.int32)


def block_scale(rng, dims, pieces, smallest, top_value):
    factor_of, own = 1.0, jax.random.fold_in(rng, 6)
    for axis_at, blocks in pieces:
        heights = jnp.exp(jax.random.uniform(jax.random.fold_in(own, axis_at), (blocks,), jnp.float32, smallest / len(pieces), top_value / len(pieces)))
        factor_of = factor_of * jnp.repeat(heights, dims[axis_at] // blocks).reshape([-1 if axis == axis_at else 1 for axis in range(len(dims))])
    return factor_of


def profile(number_of, total, bound, lean):
    loads = [(1 << 20) // math.isqrt(grade ** lean) + 1 for grade in range(2, number_of + 1)]
    rest, counts = total - bound - (number_of - 1), [1] * (number_of - 1)
    while rest > 0:
        movable = [i for i in range(number_of - 1) if counts[i] < bound]
        mass, left = sum([loads[i] for i in movable]), rest
        for i in movable:
            more = min(bound - counts[i], max(1, left * loads[i] // mass), rest)
            counts[i] = counts[i] + more
            rest = rest - more
    return np.array([bound] + counts)


def ragged_sizes(own_key, count, total, reach, slope):
    if count == 2:
        one = jax.random.randint(own_key, (), max(1, total - reach), min(reach, total - 1) + 1)
        return jnp.stack([one, total - one])
    sizes = jnp.asarray(profile(count, total, reach, slope), jnp.int32)
    twos = (count - 1) // 2
    donor, sink = sizes[1:1 + 2 * twos:2], sizes[2:2 + 2 * twos:2]
    slack = jnp.minimum(donor - 1, reach - sink)
    shifted = jax.random.randint(jax.random.fold_in(own_key, 1), (twos,), 0, 1 << 20) % (slack + 1)
    sizes = sizes.at[1:1 + 2 * twos:2].set(donor - shifted).at[2:2 + 2 * twos:2].set(sink + shifted)
    return sizes[jax.random.permutation(jax.random.fold_in(own_key, 2), count)]


def noise(own_key, shape, spread, reach, cuts=(), held_as=jnp.bfloat16):
    array = spread * jax.random.normal(own_key, shape, jnp.float32)
    if cuts:
        array = array * block_scale(own_key, shape, cuts, -0.22, 0.18)
    return jnp.clip(array, -reach, reach).astype(held_as)


def setup_inputs(seed: int = 0) -> dict:
    streams_of = jax.random.split(jax.random.key(seed), 5)
    fields = noise(streams_of[0], (LEVELS, N_TM * CAP, TILES, CELLS), 3.0, 18.0, ((0, 4), (1, 8)))
    lengths = ragged_sizes(streams_of[1], N_TM, STEPS, CAP, 2).astype(jnp.int32)
    owners = draw_owners(jax.random.fold_in(streams_of[4], 71), 0)
    thickness = jnp.clip(jnp.exp(jax.random.uniform(streams_of[3], (LEVELS,), jnp.float32, math.log(0.2), math.log(5.0))), 0.2, 5.0)
    return {"fields": fields, "lengths": lengths, "owners": owners, "thickness": thickness}


def slot_table(owners):
    tile_count = owners.shape[0]
    tile_ids = jnp.arange(tile_count, dtype=jnp.int32)
    earlier = (owners[None, :] == owners[:, None]) & (tile_ids[None, :] < tile_ids[:, None])
    tile_rank = jnp.sum(earlier.astype(jnp.int32), axis=1).astype(jnp.int32)
    position = (owners * MAXT + tile_rank).astype(jnp.int32)
    slot_ids = jnp.arange(N_TM * MAXT, dtype=jnp.int32)
    matches = (position[None, :] == slot_ids[:, None]).astype(jnp.int32)
    tile_of = jnp.sum(matches * tile_ids[None, :], axis=1).astype(jnp.int32)
    slot_valid = jnp.sum(matches, axis=1).astype(jnp.int32)
    return tile_of, slot_valid


def reference(fields, lengths, owners, thickness):
    offsets = (jnp.cumsum(lengths) - lengths).astype(jnp.int32)
    row_ids = jnp.arange(N_TM * CAP, dtype=jnp.int32)
    source_ids = row_ids // CAP
    slot_ids = row_ids % CAP
    hour_of = offsets[source_ids] + slot_ids
    is_valid = slot_ids < lengths[source_ids]
    day_ids = jnp.arange(DAYS, dtype=jnp.int32)
    select = (is_valid[:, None] & (hour_of[:, None] // 24 == day_ids[None, :])).astype(jnp.bfloat16)
    tile_of, slot_valid = slot_table(owners)
    keep = slot_valid.astype(jnp.float32)[:, None, None] / 24.0

    def level_means(level_fields):
        flat = level_fields.reshape(N_TM * CAP, TILES * CELLS)
        day_sums = jnp.dot(select.T, flat, preferred_element_type=jnp.float32)
        day_sums = day_sums.reshape(DAYS, TILES, CELLS)
        picked = jnp.take(day_sums, tile_of, axis=1)
        return jnp.transpose(picked, (1, 0, 2)) * keep

    daily_means = lax.map(level_means, fields)
    fraction = thickness / jnp.sum(thickness)
    column_means = jnp.sum(fraction[:, None, None, None] * daily_means, axis=0)
    return daily_means, column_means
```

```python
import functools

import jax
import jax.numpy as jnp
from jax import lax
from jax.experimental import pallas as pl
from jax.experimental.pallas import tpu as pltpu
from jax.sharding import PartitionSpec as P

MAXT = 2
HOURS_DEV = 3
LANES = 128
SUBS = 8
TOP_BIT = 14.98


def slot_table(owners, slot_total):
    tile_count = owners.shape[0]
    tile_ids = jnp.arange(tile_count, dtype=jnp.int32)
    earlier = (owners[None, :] == owners[:, None]) & (tile_ids[None, :] < tile_ids[:, None])
    tile_rank = jnp.sum(earlier.astype(jnp.int32), axis=1)
    position = owners * MAXT + tile_rank
    slot_ids = jnp.arange(slot_total, dtype=jnp.int32)
    matches = (position[None, :] == slot_ids[:, None]).astype(jnp.int32)
    tile_of = jnp.sum(matches * tile_ids[None, :], axis=1)
    slot_valid = jnp.sum(matches, axis=1)
    return (tile_of, slot_valid)


def many_days(fields, lengths, owners, thickness):
    local_block = fields[0]
    slot_count = local_block.shape[0]
    devices = lax.axis_size("tm")
    my_index = lax.axis_index("tm")
    all_lengths = lax.all_gather(lengths, "tm", axis=0, tiled=True)
    offsets = jnp.cumsum(all_lengths) - all_lengths
    tile_of, slot_valid = slot_table(owners, devices * MAXT)
    own_slots = lax.dynamic_slice_in_dim(slot_valid, my_index * MAXT, MAXT, 0).astype(jnp.float32)
    day_ids = jnp.arange(devices * HOURS_DEV // 24, dtype=jnp.int32)
    row_ids = jnp.arange(devices * slot_count, dtype=jnp.int32)
    source_ids = row_ids // slot_count
    slot_ids = row_ids % slot_count
    hour_of = offsets[source_ids] + slot_ids
    is_valid = slot_ids < all_lengths[source_ids]
    select = (is_valid[:, None] & (hour_of[:, None] // 24 == day_ids[None, :])).astype(jnp.bfloat16)
    outgoing = jnp.take(local_block, tile_of, axis=1)
    period_means = (
        jnp.einsum(
            "rd,rmc->mdc",
            select,
            lax.all_to_all(outgoing, "tm", split_axis=1, concat_axis=0, tiled=True),
            preferred_element_type=jnp.float32,
        )
        / 24.0
    )
    period_means = period_means * own_slots[:, None, None]
    my_level = lax.axis_index("lev")
    fraction = thickness[my_level] / jnp.sum(thickness)
    weighted = fraction * period_means
    column_sum = lax.psum(weighted, "lev")
    share = column_sum.shape[2] // lax.axis_size("lev")
    column_part = lax.dynamic_slice_in_dim(column_sum, my_level * share, share, 2)
    return (period_means[None], column_part)


def partner(index, step, size):
    if size & (size - 1) == 0:
        return index ^ step
    return lax.rem(index + step, size)


def sum_hours_kernel(devices, hours, lengths_ref, owners_ref, x_ref, own_ref, *rest):
    sends, (coded, exps) = rest[:-2], rest[-2:]
    tiles = x_ref.shape[0]
    rows = own_ref.shape[1]
    me = lax.axis_index("tm")
    held = lengths_ref[0]
    block = lax.broadcasted_iota(jnp.int32, (rows, rows * hours), 0)
    place = lax.broadcasted_iota(jnp.int32, (rows, rows * hours), 1) - block * hours
    select = jnp.where((place >= 0) & (place < jnp.minimum(held, hours)), 1.0, 0.0).astype(jnp.bfloat16)
    coded[...] = jnp.zeros_like(coded)
    exps[...] = jnp.zeros_like(exps)
    own_ref[...] = jnp.zeros_like(own_ref)
    owner = [owners_ref[t] for t in range(tiles)]
    for t in range(tiles):
        rank = jnp.int32(0)
        for u in range(t):
            rank = rank + jnp.where(owner[u] == owner[t], 1, 0)
        ahead = owner[t] - me
        slot = jnp.where(ahead < 0, ahead + devices, ahead) * MAXT + rank
        part = jnp.dot(select, x_ref[t], preferred_element_type=jnp.float32)
        cells = part.reshape(rows // SUBS, SUBS, LANES)
        top = jnp.max(jnp.abs(cells), axis=0)
        power = jnp.clip(jnp.floor(TOP_BIT - jnp.log2(top)), -126.0, 126.0)
        exps[slot] = power.astype(jnp.int32)
        code = jnp.round(cells * jnp.exp2(power)[None])
        coded[slot] = code.reshape(rows, LANES).astype(jnp.int32).astype(jnp.int16)

        @pl.when(ahead == 0)
        def _():
            own_ref[rank] = part

    for step in range(1, devices):
        send = sends[step - 1]
        for r in range(MAXT):
            send[r * rows : (r + 1) * rows, :] = coded[step * MAXT + r]
        pair = [exps[step * MAXT + r] for r in range(MAXT)]
        send[MAXT * rows :, :] = jnp.concatenate(pair, axis=0).astype(jnp.int16)


def daily_kernel(levels, thickness_ref, own_ref, *rest):
    received = rest[: -(levels + 1) - 1]
    daily_ref, shares, weighted = rest[-(levels + 1) - 1], rest[-(levels + 1) : -1], rest[-1]
    rows = own_ref.shape[1]
    part = rows // levels
    my_level = lax.axis_index("lev")
    total = thickness_ref[0]
    for level in range(1, levels):
        total = total + thickness_ref[level]
    wide = jnp.full((SUBS, LANES), thickness_ref[my_level]) / jnp.full((SUBS, LANES), total)
    for r in range(MAXT):
        cells = own_ref[r].reshape(rows // SUBS, SUBS, LANES)
        for message in received:
            first = MAXT * rows + r * SUBS
            power = message[MAXT * rows :, :].astype(jnp.float32)[r * SUBS : (r + 1) * SUBS]
            code = message[r * rows : (r + 1) * rows, :].astype(jnp.float32)
            cells = cells + code.reshape(rows // SUBS, SUBS, LANES) * jnp.exp2(-power)[None]
        cells = cells * (1.0 / 24.0)
        daily_ref[r] = cells.reshape(rows, LANES)
        weighted[r] = (cells * wide[None]).reshape(rows, LANES)
    for step in range(levels):
        start = pl.multiple_of(partner(my_level, step, levels) * part, SUBS)
        shares[step][...] = weighted[:, pl.ds(start, part), :]


def column_kernel(*refs):
    total = refs[0][...]
    for ref in refs[1:-1]:
        total = total + ref[...]
    refs[-1][...] = total


def one_day(fields, lengths, owners, thickness):
    _, hours, tiles, cells = fields.shape
    devices, levels = lax.axis_size("tm"), lax.axis_size("lev")
    rows = cells // LANES
    flat = fields[0].reshape(hours, tiles, rows, LANES).transpose(1, 2, 0, 3).reshape(tiles, rows * hours, LANES)
    vmem, smem = pl.BlockSpec(memory_space=pltpu.VMEM), pl.BlockSpec(memory_space=pltpu.SMEM)
    message = jax.ShapeDtypeStruct((MAXT * (rows + SUBS), LANES), jnp.int16)
    slots = devices * MAXT
    own, *sends = pl.pallas_call(
        functools.partial(sum_hours_kernel, devices, hours),
        out_shape=[jax.ShapeDtypeStruct((MAXT, rows, LANES), jnp.float32)] + [message] * (devices - 1),
        in_specs=[smem, smem, vmem],
        out_specs=[vmem] * devices,
        scratch_shapes=[pltpu.VMEM((slots, rows, LANES), jnp.int16), pltpu.VMEM((slots, SUBS, LANES), jnp.int32)],
    )(lengths, owners, flat)
    received = []
    for step in range(1, devices):
        pairs = [(source, (source + step) % devices) for source in range(devices)]
        received.append(lax.ppermute(sends[step - 1], "tm", pairs))
    share = jax.ShapeDtypeStruct((MAXT, rows // levels, LANES), jnp.float32)
    daily, *shares = pl.pallas_call(
        functools.partial(daily_kernel, levels),
        out_shape=[jax.ShapeDtypeStruct((MAXT, rows, LANES), jnp.float32)] + [share] * levels,
        in_specs=[smem] + [vmem] * devices,
        out_specs=[vmem] * (levels + 1),
        scratch_shapes=[pltpu.VMEM((MAXT, rows, LANES), jnp.float32)],
    )(thickness, own, *received)
    terms = [shares[0]]
    for step in range(1, levels):
        if levels & (levels - 1) == 0:
            pairs = [(source, source ^ step) for source in range(levels)]
        else:
            pairs = [(source, (source + step) % levels) for source in range(levels)]
        terms.append(lax.ppermute(shares[step], "lev", pairs))
    column = pl.pallas_call(
        column_kernel, out_shape=share, in_specs=[vmem] * levels, out_specs=vmem
    )(*terms)
    return daily.reshape(1, MAXT, 1, cells), column.reshape(MAXT, 1, cells // levels)


def solution(mesh):
    days = mesh.shape["tm"] * HOURS_DEV // 24
    placed = (P("lev", "tm", None, None), P("tm"), P(), P())
    return jax.shard_map(
        one_day if days == 1 else many_days,
        mesh=mesh,
        in_specs=placed,
        out_specs=(P("lev", "tm", None, None), P("tm", None, "lev")),
        check_vma=False,
    )
```

```python
import functools

import jax
import jax.numpy as jnp
from jax import lax
from jax.experimental import pallas as pl
from jax.experimental.pallas import tpu as pltpu
from jax.sharding import PartitionSpec as P

MAXT = 2
HOURS_DEV = 3
LANES = 128
SUBS = 8
TOP_BIT = 14.98


def slot_table(owners, slot_total):
    tile_count = owners.shape[0]
    tile_ids = jnp.arange(tile_count, dtype=jnp.int32)
    earlier = (owners[None, :] == owners[:, None]) & (tile_ids[None, :] < tile_ids[:, None])
    tile_rank = jnp.sum(earlier.astype(jnp.int32), axis=1)
    position = owners * MAXT + tile_rank
    slot_ids = jnp.arange(slot_total, dtype=jnp.int32)
    matches = (position[None, :] == slot_ids[:, None]).astype(jnp.int32)
    tile_of = jnp.sum(matches * tile_ids[None, :], axis=1)
    slot_valid = jnp.sum(matches, axis=1)
    return (tile_of, slot_valid)


def many_days(fields, lengths, owners, thickness):
    local_block = fields[0]
    slot_count = local_block.shape[0]
    devices = lax.axis_size("tm")
    my_index = lax.axis_index("tm")
    all_lengths = lax.all_gather(lengths, "tm", axis=0, tiled=True)
    offsets = jnp.cumsum(all_lengths) - all_lengths
    tile_of, slot_valid = slot_table(owners, devices * MAXT)
    own_slots = lax.dynamic_slice_in_dim(slot_valid, my_index * MAXT, MAXT, 0).astype(jnp.float32)
    day_ids = jnp.arange(devices * HOURS_DEV // 24, dtype=jnp.int32)
    row_ids = jnp.arange(devices * slot_count, dtype=jnp.int32)
    source_ids = row_ids // slot_count
    slot_ids = row_ids % slot_count
    hour_of = offsets[source_ids] + slot_ids
    is_valid = slot_ids < all_lengths[source_ids]
    select = (is_valid[:, None] & (hour_of[:, None] // 24 == day_ids[None, :])).astype(jnp.bfloat16)
    outgoing = jnp.take(local_block, tile_of, axis=1)
    period_means = (
        jnp.einsum(
            "rd,rmc->mdc",
            select,
            lax.all_to_all(outgoing, "tm", split_axis=1, concat_axis=0, tiled=True),
            preferred_element_type=jnp.float32,
        )
        / 24.0
    )
    period_means = period_means * own_slots[:, None, None]
    my_level = lax.axis_index("lev")
    fraction = thickness[my_level] / jnp.sum(thickness)
    weighted = fraction * period_means
    column_sum = lax.psum(weighted, "lev")
    share = column_sum.shape[2] // lax.axis_size("lev")
    column_part = lax.dynamic_slice_in_dim(column_sum, my_level * share, share, 2)
    return (period_means[None], column_part)


def partner(index, step, size):
    if size & (size - 1) == 0:
        return index ^ step
    return lax.rem(index + step, size)


def send_order(size):
    half = size // 2
    steps = list(range(1, size))
    if size == 8:
        return [3, 5, 4, 6, 2, 1, 7]
    return sorted(steps, key=lambda step: abs(step - half))


def sum_hours_kernel(devices, hours, lengths_hbm, owners_hbm, x_hbm, own_ref, *rest):
    sends = rest[: devices - 1]
    coded, exps, x_ref, lengths_ref, owners_ref, scalar_sem, tile_sem = rest[devices - 1 :]
    tiles = x_ref.shape[0]
    rows = own_ref.shape[1]
    loads = [pltpu.make_async_copy(x_hbm.at[t], x_ref.at[t], tile_sem.at[t]) for t in range(tiles)]
    scalars = [
        pltpu.make_async_copy(lengths_hbm, lengths_ref, scalar_sem.at[0]),
        pltpu.make_async_copy(owners_hbm, owners_ref, scalar_sem.at[1]),
    ]
    for copy in scalars + loads:
        copy.start()
    coded[...] = jnp.zeros_like(coded)
    exps[...] = jnp.zeros_like(exps)
    own_ref[...] = jnp.zeros_like(own_ref)
    me = lax.axis_index("tm")
    for copy in scalars:
        copy.wait()
    held = lengths_ref[...]
    block = lax.broadcasted_iota(jnp.int32, (rows, rows * hours), 0)
    place = lax.broadcasted_iota(jnp.int32, (rows, rows * hours), 1) - block * hours
    select = jnp.where((place >= 0) & (place < jnp.minimum(held, hours)), 1.0, 0.0).astype(jnp.bfloat16)
    owner = [owners_ref[t] for t in range(tiles)]
    for t in range(tiles):
        rank = jnp.int32(0)
        for u in range(t):
            rank = rank + jnp.where(owner[u] == owner[t], 1, 0)
        ahead = owner[t] - me
        slot = jnp.where(ahead < 0, ahead + devices, ahead) * MAXT + rank
        loads[t].wait()
        part = jnp.dot(select, x_ref[t], preferred_element_type=jnp.float32)
        cells = part.reshape(rows // SUBS, SUBS, LANES)
        top = jnp.max(jnp.abs(cells), axis=0)
        power = jnp.clip(jnp.floor(TOP_BIT - jnp.log2(top)), -126.0, 126.0)
        exps[slot] = power.astype(jnp.int32)
        code = jnp.round(cells * jnp.exp2(power)[None])
        coded[slot] = code.reshape(rows, LANES).astype(jnp.int32).astype(jnp.int16)

        @pl.when(ahead == 0)
        def _():
            own_ref[rank] = part

    for step in range(1, devices):
        send = sends[step - 1]
        for r in range(MAXT):
            send[r * rows : (r + 1) * rows, :] = coded[step * MAXT + r]
        pair = [exps[step * MAXT + r] for r in range(MAXT)]
        send[MAXT * rows :, :] = jnp.concatenate(pair, axis=0).astype(jnp.int16)


def daily_kernel(levels, thickness_ref, own_ref, *rest):
    received = rest[: -(levels + 1) - 1]
    daily_ref, shares, weighted = rest[-(levels + 1) - 1], rest[-(levels + 1) : -1], rest[-1]
    rows = own_ref.shape[1]
    part = rows // levels
    my_level = lax.axis_index("lev")
    total = thickness_ref[0]
    for level in range(1, levels):
        total = total + thickness_ref[level]
    wide = jnp.full((SUBS, LANES), thickness_ref[my_level]) / jnp.full((SUBS, LANES), total)
    for r in range(MAXT):
        cells = own_ref[r].reshape(rows // SUBS, SUBS, LANES)
        for message in received:
            first = MAXT * rows + r * SUBS
            power = message[MAXT * rows :, :].astype(jnp.float32)[r * SUBS : (r + 1) * SUBS]
            code = message[r * rows : (r + 1) * rows, :].astype(jnp.float32)
            cells = cells + code.reshape(rows // SUBS, SUBS, LANES) * jnp.exp2(-power)[None]
        cells = cells * (1.0 / 24.0)
        daily_ref[r] = cells.reshape(rows, LANES)
        weighted[r] = (cells * wide[None]).reshape(rows, LANES)
    for step in range(levels):
        start = pl.multiple_of(partner(my_level, step, levels) * part, SUBS)
        shares[step][...] = weighted[:, pl.ds(start, part), :]


def column_kernel(*refs):
    total = refs[0][...]
    for ref in refs[1:-1]:
        total = total + ref[...]
    refs[-1][...] = total


def one_day(fields, lengths, owners, thickness):
    _, hours, tiles, cells = fields.shape
    devices, levels = lax.axis_size("tm"), lax.axis_size("lev")
    rows = cells // LANES
    flat = fields[0].reshape(hours, tiles, rows, LANES).transpose(1, 2, 0, 3).reshape(tiles, rows * hours, LANES)
    hbm = pl.BlockSpec(memory_space=pltpu.HBM)
    flat = pltpu.with_memory_space_constraint(flat, pltpu.HBM)
    owners = pltpu.with_memory_space_constraint(owners, pltpu.HBM)
    vmem, smem = pl.BlockSpec(memory_space=pltpu.VMEM), pl.BlockSpec(memory_space=pltpu.SMEM)
    message = jax.ShapeDtypeStruct((MAXT * (rows + SUBS), LANES), jnp.int16)
    slots = devices * MAXT
    own, *sends = pl.pallas_call(
        functools.partial(sum_hours_kernel, devices, hours),
        out_shape=[jax.ShapeDtypeStruct((MAXT, rows, LANES), jnp.float32)] + [message] * (devices - 1),
        in_specs=[hbm] * 3,
        out_specs=[vmem] * devices,
        scratch_shapes=[
            pltpu.VMEM((slots, rows, LANES), jnp.int16),
            pltpu.VMEM((slots, SUBS, LANES), jnp.int32),
            pltpu.VMEM(flat.shape, flat.dtype),
            pltpu.VMEM((1, 1), lengths.dtype),
            pltpu.SMEM(owners.shape, owners.dtype),
            pltpu.SemaphoreType.DMA((2,)),
            pltpu.SemaphoreType.DMA((tiles,)),
        ],
        compiler_params=pltpu.CompilerParams(vmem_limit_bytes=8 << 20),
    )(lengths[None], owners, flat)
    received = []
    for step in send_order(devices):
        pairs = [(source, (source + step) % devices) for source in range(devices)]
        received.append(lax.ppermute(sends[step - 1], "tm", pairs))
    share = jax.ShapeDtypeStruct((MAXT, rows // levels, LANES), jnp.float32)
    daily, *shares = pl.pallas_call(
        functools.partial(daily_kernel, levels),
        out_shape=[jax.ShapeDtypeStruct((MAXT, rows, LANES), jnp.float32)] + [share] * levels,
        in_specs=[smem] + [vmem] * devices,
        out_specs=[vmem] * (levels + 1),
        scratch_shapes=[pltpu.VMEM((MAXT, rows, LANES), jnp.float32)],
        compiler_params=pltpu.CompilerParams(vmem_limit_bytes=8 << 20),
    )(thickness, own, *received)
    terms = [shares[0]]
    for step in range(1, levels):
        if levels & (levels - 1) == 0:
            pairs = [(source, source ^ step) for source in range(levels)]
        else:
            pairs = [(source, (source + step) % levels) for source in range(levels)]
        terms.append(lax.ppermute(shares[step], "lev", pairs))
    column = pl.pallas_call(
        column_kernel,
        out_shape=share,
        in_specs=[vmem] * levels,
        out_specs=vmem,
        compiler_params=pltpu.CompilerParams(vmem_limit_bytes=8 << 20),
    )(*terms)
    return daily.reshape(1, MAXT, 1, cells), column.reshape(MAXT, 1, cells // levels)


def solution(mesh):
    days = mesh.shape["tm"] * HOURS_DEV // 24
    placed = (P("lev", "tm", None, None), P("tm"), P(), P())
    return jax.shard_map(
        one_day if days == 1 else many_days,
        mesh=mesh,
        in_specs=placed,
        out_specs=(P("lev", "tm", None, None), P("tm", None, "lev")),
        check_vma=False,
    )
```

```python
import functools

import jax
import jax.numpy as jnp
from jax import lax
from jax.experimental import pallas as pl
from jax.experimental.pallas import tpu as pltpu
from jax.sharding import PartitionSpec as P

MAXT = 2
HOURS_DEV = 3
LANES = 128
SUBS = 8
TOP_BIT = 14.98
GROUP = 3


def slot_table(owners, slot_total):
    tile_count = owners.shape[0]
    tile_ids = jnp.arange(tile_count, dtype=jnp.int32)
    earlier = (owners[None, :] == owners[:, None]) & (tile_ids[None, :] < tile_ids[:, None])
    tile_rank = jnp.sum(earlier.astype(jnp.int32), axis=1)
    position = owners * MAXT + tile_rank
    slot_ids = jnp.arange(slot_total, dtype=jnp.int32)
    matches = (position[None, :] == slot_ids[:, None]).astype(jnp.int32)
    tile_of = jnp.sum(matches * tile_ids[None, :], axis=1)
    slot_valid = jnp.sum(matches, axis=1)
    return (tile_of, slot_valid)


def many_days(fields, lengths, owners, thickness):
    local_block = fields[0]
    slot_count = local_block.shape[0]
    devices = lax.axis_size("tm")
    my_index = lax.axis_index("tm")
    all_lengths = lax.all_gather(lengths, "tm", axis=0, tiled=True)
    offsets = jnp.cumsum(all_lengths) - all_lengths
    tile_of, slot_valid = slot_table(owners, devices * MAXT)
    own_slots = lax.dynamic_slice_in_dim(slot_valid, my_index * MAXT, MAXT, 0).astype(jnp.float32)
    day_ids = jnp.arange(devices * HOURS_DEV // 24, dtype=jnp.int32)
    row_ids = jnp.arange(devices * slot_count, dtype=jnp.int32)
    source_ids = row_ids // slot_count
    slot_ids = row_ids % slot_count
    hour_of = offsets[source_ids] + slot_ids
    is_valid = slot_ids < all_lengths[source_ids]
    select = (is_valid[:, None] & (hour_of[:, None] // 24 == day_ids[None, :])).astype(jnp.bfloat16)
    outgoing = jnp.take(local_block, tile_of, axis=1)
    period_means = (
        jnp.einsum(
            "rd,rmc->mdc",
            select,
            lax.all_to_all(outgoing, "tm", split_axis=1, concat_axis=0, tiled=True),
            preferred_element_type=jnp.float32,
        )
        / 24.0
    )
    period_means = period_means * own_slots[:, None, None]
    my_level = lax.axis_index("lev")
    fraction = thickness[my_level] / jnp.sum(thickness)
    weighted = fraction * period_means
    column_sum = lax.psum(weighted, "lev")
    share = column_sum.shape[2] // lax.axis_size("lev")
    column_part = lax.dynamic_slice_in_dim(column_sum, my_level * share, share, 2)
    return (period_means[None], column_part)


def partner(index, step, size):
    if size & (size - 1) == 0:
        return index ^ step
    return lax.rem(index + step, size)


def send_order(size):
    half = size // 2
    steps = list(range(1, size))
    if size == 8:
        return [3, 5, 4, 6, 2, 1, 7]
    return sorted(steps, key=lambda step: abs(step - half))


def sum_hours_kernel(devices, hours, levels, lengths_ref, owners_hbm, thickness_hbm, x_hbm, *rest):
    sends, share_ref = rest[:devices], rest[devices]
    coded, exps, x_ref, owners_ref, thickness_ref, scalar_sem, tile_sem = rest[devices + 1 :]
    tiles = x_ref.shape[0]
    rows = x_ref.shape[1] // hours
    half = rows // 2
    loads = [pltpu.make_async_copy(x_hbm.at[t], x_ref.at[t], tile_sem.at[t]) for t in range(tiles)]
    scalars = [
        pltpu.make_async_copy(owners_hbm, owners_ref, scalar_sem.at[0]),
        pltpu.make_async_copy(thickness_hbm, thickness_ref, scalar_sem.at[1]),
    ]
    for copy in scalars + loads:
        copy.start()
    coded[...] = jnp.zeros_like(coded)
    exps[...] = jnp.zeros_like(exps)
    me = lax.axis_index("tm")
    held = jnp.minimum(lengths_ref[0], hours)
    block = lax.broadcasted_iota(jnp.int32, (half, half * hours), 0)
    place = lax.broadcasted_iota(jnp.int32, (half, half * hours), 1) - block * hours
    select = jnp.where((place >= 0) & (place < held), 1.0, 0.0).astype(jnp.bfloat16)
    for copy in scalars:
        copy.wait()
    total = thickness_ref[0]
    for level in range(1, levels):
        total = total + thickness_ref[level]
    mine = jnp.full((SUBS, LANES), thickness_ref[lax.axis_index("lev")])
    share_ref[...] = mine / jnp.full((SUBS, LANES), total)
    owner = [owners_ref[t] for t in range(tiles)]
    slots = []
    for t in range(tiles):
        rank = jnp.int32(0)
        for u in range(t):
            rank = rank + jnp.where(owner[u] == owner[t], 1, 0)
        ahead = owner[t] - me
        slots.append(jnp.where(ahead < 0, ahead + devices, ahead) * MAXT + rank)
    for first in range(0, tiles, GROUP):
        group = range(first, min(first + GROUP, tiles))
        for t in group:
            loads[t].wait()
        for t in group:
            top = None
            parts = []
            for h in range(2):
                x = x_ref[t, h * half * hours : (h + 1) * half * hours, :]
                part = jnp.dot(select, x, preferred_element_type=jnp.float32)
                part = part.reshape(half // SUBS, SUBS, LANES)
                parts.append(part)
                peak = jnp.max(jnp.abs(part), axis=0)
                top = peak if top is None else jnp.maximum(top, peak)
            power = jnp.clip(jnp.floor(TOP_BIT - jnp.log2(top)), -126.0, 126.0)
            scale = jnp.exp2(power)
            exps[slots[t]] = power.astype(jnp.int32)
            for h in range(2):
                code = jnp.round(parts[h] * scale[None]).reshape(half, LANES)
                coded[slots[t], h * half : (h + 1) * half, :] = code.astype(jnp.int32).astype(jnp.int16)
    for step in range(devices):
        send = sends[step]
        for r in range(MAXT):
            send[r * rows : (r + 1) * rows, :] = coded[step * MAXT + r]
        pair = [exps[step * MAXT + r] for r in range(MAXT)]
        send[MAXT * rows :, :] = jnp.concatenate(pair, axis=0).astype(jnp.int16)


def daily_kernel(devices, levels, share_ref, *rest):
    received, daily_ref = rest[:devices], rest[devices]
    shares, weighted = rest[devices + 1 : -1], rest[-1]
    rows = weighted.shape[1]
    part = rows // levels
    my_level = lax.axis_index("lev")
    share = share_ref[...]
    inverse = [jnp.exp2(-message[MAXT * rows :, :].astype(jnp.float32)) for message in received]
    for r in range(MAXT):
        cells = None
        for message, scale in zip(received, inverse):
            code = message[r * rows : (r + 1) * rows, :].astype(jnp.float32)
            term = code.reshape(rows // SUBS, SUBS, LANES) * scale[r * SUBS : (r + 1) * SUBS][None]
            cells = term if cells is None else cells + term
        cells = cells * (1.0 / 24.0)
        daily_ref[r] = cells.reshape(rows, LANES)
        weighted[r] = (cells * share[None]).reshape(rows, LANES)
    for step in range(levels):
        start = pl.multiple_of(partner(my_level, step, levels) * part, SUBS)
        shares[step][...] = weighted[:, pl.ds(start, part), :]


def column_kernel(*refs):
    total = refs[0][...]
    for ref in refs[1:-1]:
        total = total + ref[...]
    refs[-1][...] = total


def one_day(fields, lengths, owners, thickness):
    _, hours, tiles, cells = fields.shape
    devices, levels = lax.axis_size("tm"), lax.axis_size("lev")
    rows = cells // LANES
    flat = fields[0].reshape(hours, tiles, rows, LANES).transpose(1, 2, 0, 3).reshape(tiles, rows * hours, LANES)
    flat, owners, thickness = (pltpu.with_memory_space_constraint(x, pltpu.HBM) for x in (flat, owners, thickness))
    hbm = pl.BlockSpec(memory_space=pltpu.HBM)
    vmem, smem = pl.BlockSpec(memory_space=pltpu.VMEM), pl.BlockSpec(memory_space=pltpu.SMEM)
    message = jax.ShapeDtypeStruct((MAXT * (rows + SUBS), LANES), jnp.int16)
    slots = devices * MAXT
    *messages, weight = pl.pallas_call(
        functools.partial(sum_hours_kernel, devices, hours, levels),
        out_shape=[message] * devices + [jax.ShapeDtypeStruct((SUBS, LANES), jnp.float32)],
        in_specs=[smem, hbm, hbm, hbm],
        out_specs=[vmem] * (devices + 1),
        scratch_shapes=[
            pltpu.VMEM((slots, rows, LANES), jnp.int16),
            pltpu.VMEM((slots, SUBS, LANES), jnp.int32),
            pltpu.VMEM(flat.shape, flat.dtype),
            pltpu.SMEM(owners.shape, owners.dtype),
            pltpu.SMEM(thickness.shape, thickness.dtype),
            pltpu.SemaphoreType.DMA((2,)),
            pltpu.SemaphoreType.DMA((tiles,)),
        ],
        compiler_params=pltpu.CompilerParams(vmem_limit_bytes=8 << 20),
    )(lengths, owners, thickness, flat)
    received = [messages[0]]
    for step in send_order(devices):
        pairs = [(source, (source + step) % devices) for source in range(devices)]
        received.append(lax.ppermute(messages[step], "tm", pairs))
    share = jax.ShapeDtypeStruct((MAXT, rows // levels, LANES), jnp.float32)
    daily, *shares = pl.pallas_call(
        functools.partial(daily_kernel, devices, levels),
        out_shape=[pltpu.VMEM((MAXT, rows, LANES), jnp.float32)] + [share] * levels,
        in_specs=[vmem] * (devices + 1),
        out_specs=[vmem] * (levels + 1),
        scratch_shapes=[pltpu.VMEM((MAXT, rows, LANES), jnp.float32)],
        compiler_params=pltpu.CompilerParams(vmem_limit_bytes=8 << 20),
    )(weight, *received)
    terms = [shares[0]]
    for step in range(1, levels):
        if levels & (levels - 1) == 0:
            pairs = [(source, source ^ step) for source in range(levels)]
        else:
            pairs = [(source, (source + step) % levels) for source in range(levels)]
        terms.append(lax.ppermute(shares[step], "lev", pairs))
    column = pl.pallas_call(
        column_kernel,
        out_shape=share,
        in_specs=[vmem] * levels,
        out_specs=vmem,
        compiler_params=pltpu.CompilerParams(vmem_limit_bytes=8 << 20),
    )(*terms)
    return daily.reshape(1, MAXT, 1, cells), column.reshape(MAXT, 1, cells // levels)


def solution(mesh):
    days = mesh.shape["tm"] * HOURS_DEV // 24
    placed = (P("lev", "tm", None, None), P("tm"), P(), P())
    return jax.shard_map(
        one_day if days == 1 else many_days,
        mesh=mesh,
        in_specs=placed,
        out_specs=(P("lev", "tm", None, None), P("tm", None, "lev")),
        check_vma=False,
    )
```

```python
import functools

import jax
import jax.numpy as jnp
from jax import lax
from jax.experimental import pallas as pl
from jax.experimental.pallas import tpu as pltpu
from jax.sharding import PartitionSpec as P

MAXT = 2
HOURS_DEV = 3
LANES = 128
SUBS = 8
TOP_BIT = 14.98


def slot_table(owners, slot_total):
    tile_count = owners.shape[0]
    tile_ids = jnp.arange(tile_count, dtype=jnp.int32)
    earlier = (owners[None, :] == owners[:, None]) & (tile_ids[None, :] < tile_ids[:, None])
    tile_rank = jnp.sum(earlier.astype(jnp.int32), axis=1)
    position = owners * MAXT + tile_rank
    slot_ids = jnp.arange(slot_total, dtype=jnp.int32)
    matches = (position[None, :] == slot_ids[:, None]).astype(jnp.int32)
    tile_of = jnp.sum(matches * tile_ids[None, :], axis=1)
    slot_valid = jnp.sum(matches, axis=1)
    return (tile_of, slot_valid)


def many_days(fields, lengths, owners, thickness):
    local_block = fields[0]
    slot_count = local_block.shape[0]
    devices = lax.axis_size("tm")
    my_index = lax.axis_index("tm")
    all_lengths = lax.all_gather(lengths, "tm", axis=0, tiled=True)
    offsets = jnp.cumsum(all_lengths) - all_lengths
    tile_of, slot_valid = slot_table(owners, devices * MAXT)
    own_slots = lax.dynamic_slice_in_dim(slot_valid, my_index * MAXT, MAXT, 0).astype(jnp.float32)
    day_ids = jnp.arange(devices * HOURS_DEV // 24, dtype=jnp.int32)
    row_ids = jnp.arange(devices * slot_count, dtype=jnp.int32)
    source_ids = row_ids // slot_count
    slot_ids = row_ids % slot_count
    hour_of = offsets[source_ids] + slot_ids
    is_valid = slot_ids < all_lengths[source_ids]
    select = (is_valid[:, None] & (hour_of[:, None] // 24 == day_ids[None, :])).astype(jnp.bfloat16)
    outgoing = jnp.take(local_block, tile_of, axis=1)
    period_means = (
        jnp.einsum(
            "rd,rmc->mdc",
            select,
            lax.all_to_all(outgoing, "tm", split_axis=1, concat_axis=0, tiled=True),
            preferred_element_type=jnp.float32,
        )
        / 24.0
    )
    period_means = period_means * own_slots[:, None, None]
    my_level = lax.axis_index("lev")
    fraction = thickness[my_level] / jnp.sum(thickness)
    weighted = fraction * period_means
    column_sum = lax.psum(weighted, "lev")
    share = column_sum.shape[2] // lax.axis_size("lev")
    column_part = lax.dynamic_slice_in_dim(column_sum, my_level * share, share, 2)
    return (period_means[None], column_part)


def partner(index, step, size):
    if size & (size - 1) == 0:
        return index ^ step
    return lax.rem(index + step, size)


def send_order(size):
    if size == 8:
        return [3, 5, 4, 6, 2, 1, 7]
    return list(range(1, size))


def sum_hours_kernel(devices, hours, levels, lengths_ref, owners_hbm, thickness_hbm, x_hbm, *rest):
    sends, share_ref = rest[:devices], rest[devices]
    coded, exps, x_ref, owners_ref, thickness_ref, scalar_sem, tile_sem = rest[devices + 1 :]
    tiles = x_ref.shape[0]
    rows = x_ref.shape[1] // hours
    half = rows // 2
    loads = [pltpu.make_async_copy(x_hbm.at[t], x_ref.at[t], tile_sem.at[t]) for t in range(tiles)]
    scalars = [
        pltpu.make_async_copy(owners_hbm, owners_ref, scalar_sem.at[0]),
        pltpu.make_async_copy(thickness_hbm, thickness_ref, scalar_sem.at[1]),
    ]
    for copy in scalars + loads:
        copy.start()
    coded[...] = jnp.zeros_like(coded)
    exps[...] = jnp.zeros_like(exps)
    me = lax.axis_index("tm")
    held = jnp.minimum(lengths_ref[0], hours)
    block = lax.broadcasted_iota(jnp.int32, (half, half * hours), 0)
    place = lax.broadcasted_iota(jnp.int32, (half, half * hours), 1) - block * hours
    select = jnp.where((place >= 0) & (place < held), 1.0, 0.0).astype(jnp.bfloat16)
    for copy in scalars:
        copy.wait()
    total = thickness_ref[0]
    for level in range(1, levels):
        total = total + thickness_ref[level]
    mine = jnp.full((SUBS, LANES), thickness_ref[lax.axis_index("lev")])
    share_ref[...] = mine / jnp.full((SUBS, LANES), total)
    owner = [owners_ref[t] for t in range(tiles)]
    slots = []
    for t in range(tiles):
        rank = jnp.int32(0)
        for u in range(t):
            rank = rank + jnp.where(owner[u] == owner[t], 1, 0)
        ahead = owner[t] - me
        slots.append(jnp.where(ahead < 0, ahead + devices, ahead) * MAXT + rank)
    for copy in loads:
        copy.wait()
    for t in range(tiles):
        top = None
        parts = []
        for h in range(2):
            x = x_ref[t, h * half * hours : (h + 1) * half * hours, :]
            part = jnp.dot(select, x, preferred_element_type=jnp.float32)
            part = part.reshape(half // SUBS, SUBS, LANES)
            parts.append(part)
            peak = jnp.max(jnp.abs(part), axis=0)
            top = peak if top is None else jnp.maximum(top, peak)
        top = jnp.maximum(top, pltpu.roll(top, SUBS // 2, 0))
        power = jnp.clip(jnp.floor(TOP_BIT - jnp.log2(top)), -126.0, 126.0)
        scale = jnp.exp2(power)
        exps[slots[t]] = power.astype(jnp.int32)
        for h in range(2):
            code = jnp.round(parts[h] * scale[None]).reshape(half, LANES)
            coded[slots[t], h * half : (h + 1) * half, :] = code.astype(jnp.int32).astype(jnp.int16)
    lower = lax.broadcasted_iota(jnp.int32, (SUBS, LANES), 0) < SUBS // 2
    for step in range(devices):
        send = sends[step]
        for r in range(MAXT):
            send[r * rows : (r + 1) * rows, :] = coded[step * MAXT + r]
        pair = jnp.where(lower, exps[step * MAXT], exps[step * MAXT + 1])
        send[MAXT * rows :, :] = pair.astype(jnp.int16)


def daily_kernel(devices, levels, share_ref, *rest):
    received, daily_ref = rest[:devices], rest[devices]
    shares, weighted = rest[devices + 1 : -1], rest[-1]
    rows = weighted.shape[1]
    part = rows // levels
    my_level = lax.axis_index("lev")
    share = share_ref[...]
    lower = lax.broadcasted_iota(jnp.int32, (SUBS, LANES), 0) < SUBS // 2
    inverse = []
    for message in received:
        scale = jnp.exp2(-message[MAXT * rows :, :].astype(jnp.float32))
        other = pltpu.roll(scale, SUBS // 2, 0)
        inverse.append([jnp.where(lower, scale, other), jnp.where(lower, other, scale)])
    for r in range(MAXT):
        cells = None
        for message, scale in zip(received, inverse):
            code = message[r * rows : (r + 1) * rows, :].astype(jnp.float32)
            term = code.reshape(rows // SUBS, SUBS, LANES) * scale[r][None]
            cells = term if cells is None else cells + term
        cells = cells * (1.0 / 24.0)
        daily_ref[r] = cells.reshape(rows, LANES)
        weighted[r] = (cells * share[None]).reshape(rows, LANES)
    for step in range(levels):
        start = pl.multiple_of(partner(my_level, step, levels) * part, SUBS)
        shares[step][...] = weighted[:, pl.ds(start, part), :]


def column_kernel(*refs):
    total = refs[0][...]
    for ref in refs[1:-1]:
        total = total + ref[...]
    refs[-1][...] = total


def one_day(fields, lengths, owners, thickness):
    _, hours, tiles, cells = fields.shape
    devices, levels = lax.axis_size("tm"), lax.axis_size("lev")
    rows = cells // LANES
    flat = fields[0].reshape(hours, tiles, rows, LANES).transpose(1, 2, 0, 3).reshape(tiles, rows * hours, LANES)
    flat, owners, thickness = (pltpu.with_memory_space_constraint(x, pltpu.HBM) for x in (flat, owners, thickness))
    hbm = pl.BlockSpec(memory_space=pltpu.HBM)
    vmem, smem = pl.BlockSpec(memory_space=pltpu.VMEM), pl.BlockSpec(memory_space=pltpu.SMEM)
    message = jax.ShapeDtypeStruct((MAXT * rows + SUBS, LANES), jnp.int16)
    slots = devices * MAXT
    *messages, weight = pl.pallas_call(
        functools.partial(sum_hours_kernel, devices, hours, levels),
        out_shape=[message] * devices + [jax.ShapeDtypeStruct((SUBS, LANES), jnp.float32)],
        in_specs=[smem, hbm, hbm, hbm],
        out_specs=[vmem] * (devices + 1),
        scratch_shapes=[
            pltpu.VMEM((slots, rows, LANES), jnp.int16),
            pltpu.VMEM((slots, SUBS, LANES), jnp.int32),
            pltpu.VMEM(flat.shape, flat.dtype),
            pltpu.SMEM(owners.shape, owners.dtype),
            pltpu.SMEM(thickness.shape, thickness.dtype),
            pltpu.SemaphoreType.DMA((2,)),
            pltpu.SemaphoreType.DMA((tiles,)),
        ],
        compiler_params=pltpu.CompilerParams(vmem_limit_bytes=8 << 20),
    )(lengths, owners, thickness, flat)
    received = [messages[0]]
    for step in send_order(devices):
        pairs = [(source, (source + step) % devices) for source in range(devices)]
        received.append(lax.ppermute(messages[step], "tm", pairs))
    share = jax.ShapeDtypeStruct((MAXT, rows // levels, LANES), jnp.float32)
    daily, *shares = pl.pallas_call(
        functools.partial(daily_kernel, devices, levels),
        out_shape=[pltpu.VMEM((MAXT, rows, LANES), jnp.float32)] + [share] * levels,
        in_specs=[vmem] * (devices + 1),
        out_specs=[vmem] * (levels + 1),
        scratch_shapes=[pltpu.VMEM((MAXT, rows, LANES), jnp.float32)],
        compiler_params=pltpu.CompilerParams(vmem_limit_bytes=8 << 20),
    )(weight, *received)
    terms = [shares[0]]
    for step in reversed(range(1, levels)):
        if levels & (levels - 1) == 0:
            pairs = [(source, source ^ step) for source in range(levels)]
        else:
            pairs = [(source, (source + step) % levels) for source in range(levels)]
        terms.append(lax.ppermute(shares[step], "lev", pairs))
    column = pl.pallas_call(
        column_kernel,
        out_shape=share,
        in_specs=[vmem] * levels,
        out_specs=vmem,
        compiler_params=pltpu.CompilerParams(vmem_limit_bytes=8 << 20),
    )(*terms)
    return daily.reshape(1, MAXT, 1, cells), column.reshape(MAXT, 1, cells // levels)


def solution(mesh):
    days = mesh.shape["tm"] * HOURS_DEV // 24
    placed = (P("lev", "tm", None, None), P("tm"), P(), P())
    return jax.shard_map(
        one_day if days == 1 else many_days,
        mesh=mesh,
        in_specs=placed,
        out_specs=(P("lev", "tm", None, None), P("tm", None, "lev")),
        check_vma=False,
    )
```

```python
import functools

import jax
import jax.numpy as jnp
from jax import lax
from jax.experimental import pallas as pl
from jax.experimental.pallas import tpu as pltpu
from jax.sharding import PartitionSpec as P

MAXT = 2
HOURS_DEV = 3
LANES = 128
SUBS = 8
TOP_BIT = 14.98


def slot_table(owners, slot_total):
    tile_count = owners.shape[0]
    tile_ids = jnp.arange(tile_count, dtype=jnp.int32)
    earlier = (owners[None, :] == owners[:, None]) & (tile_ids[None, :] < tile_ids[:, None])
    tile_rank = jnp.sum(earlier.astype(jnp.int32), axis=1)
    position = owners * MAXT + tile_rank
    slot_ids = jnp.arange(slot_total, dtype=jnp.int32)
    matches = (position[None, :] == slot_ids[:, None]).astype(jnp.int32)
    tile_of = jnp.sum(matches * tile_ids[None, :], axis=1)
    slot_valid = jnp.sum(matches, axis=1)
    return (tile_of, slot_valid)


def many_days(fields, lengths, owners, thickness):
    local_block = fields[0]
    slot_count = local_block.shape[0]
    devices = lax.axis_size("tm")
    my_index = lax.axis_index("tm")
    all_lengths = lax.all_gather(lengths, "tm", axis=0, tiled=True)
    offsets = jnp.cumsum(all_lengths) - all_lengths
    tile_of, slot_valid = slot_table(owners, devices * MAXT)
    own_slots = lax.dynamic_slice_in_dim(slot_valid, my_index * MAXT, MAXT, 0).astype(jnp.float32)
    day_ids = jnp.arange(devices * HOURS_DEV // 24, dtype=jnp.int32)
    row_ids = jnp.arange(devices * slot_count, dtype=jnp.int32)
    source_ids = row_ids // slot_count
    slot_ids = row_ids % slot_count
    hour_of = offsets[source_ids] + slot_ids
    is_valid = slot_ids < all_lengths[source_ids]
    select = (is_valid[:, None] & (hour_of[:, None] // 24 == day_ids[None, :])).astype(jnp.bfloat16)
    outgoing = jnp.take(local_block, tile_of, axis=1)
    period_means = (
        jnp.einsum(
            "rd,rmc->mdc",
            select,
            lax.all_to_all(outgoing, "tm", split_axis=1, concat_axis=0, tiled=True),
            preferred_element_type=jnp.float32,
        )
        / 24.0
    )
    period_means = period_means * own_slots[:, None, None]
    my_level = lax.axis_index("lev")
    fraction = thickness[my_level] / jnp.sum(thickness)
    weighted = fraction * period_means
    column_sum = lax.psum(weighted, "lev")
    share = column_sum.shape[2] // lax.axis_size("lev")
    column_part = lax.dynamic_slice_in_dim(column_sum, my_level * share, share, 2)
    return (period_means[None], column_part)


def partner(index, step, size):
    if size & (size - 1) == 0:
        return index ^ step
    return lax.rem(index + step, size)


def send_order(size):
    if size == 8:
        return [3, 4, 1, 5, 7, 2, 6]
    return list(range(1, size))


def step_to(owner, me, size):
    ahead = (owner >> 1) - (me >> 1)
    return jnp.where(ahead < 0, ahead + size // 2, ahead) * 2 + ((owner ^ me) & 1)


def target(source, step, size):
    return ((source // 2 + step // 2) % (size // 2)) * 2 + ((source ^ step) & 1)


def sum_hours_kernel(devices, hours, levels, lengths_ref, owners_hbm, thickness_hbm, x_hbm, *rest):
    sends, share_ref = rest[:devices], rest[devices]
    coded, exps, x_ref, owners_ref, thickness_ref, scalar_sem, tile_sem = rest[devices + 1 :]
    tiles = x_ref.shape[0]
    rows = x_ref.shape[1] // hours
    half = rows // 2
    loads = [pltpu.make_async_copy(x_hbm.at[t], x_ref.at[t], tile_sem.at[t]) for t in range(tiles)]
    scalars = [
        pltpu.make_async_copy(owners_hbm, owners_ref, scalar_sem.at[0]),
        pltpu.make_async_copy(thickness_hbm, thickness_ref, scalar_sem.at[1]),
    ]
    for copy in scalars + loads:
        copy.start()
    coded[...] = jnp.zeros_like(coded)
    exps[...] = jnp.zeros_like(exps)
    me = lax.axis_index("tm")
    held = jnp.minimum(lengths_ref[0], hours)
    block = lax.broadcasted_iota(jnp.int32, (half, half * hours), 0)
    place = lax.broadcasted_iota(jnp.int32, (half, half * hours), 1) - block * hours
    select = jnp.where((place >= 0) & (place < held), 1.0, 0.0).astype(jnp.bfloat16)
    for copy in scalars:
        copy.wait()
    total = thickness_ref[0]
    for level in range(1, levels):
        total = total + thickness_ref[level]
    mine = jnp.full((SUBS, LANES), thickness_ref[lax.axis_index("lev")])
    share_ref[...] = mine / jnp.full((SUBS, LANES), total)
    owner = [owners_ref[t] for t in range(tiles)]
    slots = []
    for t in range(tiles):
        rank = jnp.int32(0)
        for u in range(t):
            rank = rank + jnp.where(owner[u] == owner[t], 1, 0)
        slots.append(step_to(owner[t], me, devices) * MAXT + rank)
    for copy in loads:
        copy.wait()
    for t in range(tiles):
        top = None
        parts = []
        for h in range(2):
            x = x_ref[t, h * half * hours : (h + 1) * half * hours, :]
            part = jnp.dot(select, x, preferred_element_type=jnp.float32)
            part = part.reshape(half // SUBS, SUBS, LANES)
            parts.append(part)
            peak = jnp.max(jnp.abs(part), axis=0)
            top = peak if top is None else jnp.maximum(top, peak)
        top = jnp.maximum(top, pltpu.roll(top, SUBS // 2, 0))
        power = jnp.clip(jnp.floor(TOP_BIT - jnp.log2(top)), -126.0, 126.0)
        scale = jnp.exp2(power)
        exps[slots[t]] = power.astype(jnp.int32)
        for h in range(2):
            code = jnp.round(parts[h] * scale[None]).reshape(half, LANES)
            coded[slots[t], h * half : (h + 1) * half, :] = code.astype(jnp.int32).astype(jnp.int16)
    lower = lax.broadcasted_iota(jnp.int32, (SUBS, LANES), 0) < SUBS // 2
    for step in range(devices):
        send = sends[step]
        for r in range(MAXT):
            send[r * rows : (r + 1) * rows, :] = coded[step * MAXT + r]
        pair = jnp.where(lower, exps[step * MAXT], exps[step * MAXT + 1])
        send[MAXT * rows :, :] = pair.astype(jnp.int16)


def daily_kernel(devices, levels, share_ref, *rest):
    received, daily_ref = rest[:devices], rest[devices]
    shares, weighted = rest[devices + 1 : -1], rest[-1]
    rows = weighted.shape[1]
    part = rows // levels
    my_level = lax.axis_index("lev")
    share = share_ref[...]
    lower = lax.broadcasted_iota(jnp.int32, (SUBS, LANES), 0) < SUBS // 2
    inverse = []
    for message in received:
        scale = jnp.exp2(-message[MAXT * rows :, :].astype(jnp.float32))
        other = pltpu.roll(scale, SUBS // 2, 0)
        inverse.append([jnp.where(lower, scale, other), jnp.where(lower, other, scale)])
    for r in range(MAXT):
        cells = None
        for message, scale in zip(received, inverse):
            code = message[r * rows : (r + 1) * rows, :].astype(jnp.float32)
            term = code.reshape(rows // SUBS, SUBS, LANES) * scale[r][None]
            cells = term if cells is None else cells + term
        cells = cells * (1.0 / 24.0)
        daily_ref[r] = cells.reshape(rows, LANES)
        weighted[r] = (cells * share[None]).reshape(rows, LANES)
    for step in range(levels):
        start = pl.multiple_of(partner(my_level, step, levels) * part, SUBS)
        shares[step][...] = weighted[:, pl.ds(start, part), :]


def column_kernel(*refs):
    total = refs[0][...]
    for ref in refs[1:-1]:
        total = total + ref[...]
    refs[-1][...] = total


def one_day(fields, lengths, owners, thickness):
    _, hours, tiles, cells = fields.shape
    devices, levels = lax.axis_size("tm"), lax.axis_size("lev")
    rows = cells // LANES
    flat = fields[0].reshape(hours, tiles, rows, LANES).transpose(1, 2, 0, 3).reshape(tiles, rows * hours, LANES)
    flat, owners, thickness = (pltpu.with_memory_space_constraint(x, pltpu.HBM) for x in (flat, owners, thickness))
    hbm = pl.BlockSpec(memory_space=pltpu.HBM)
    vmem, smem = pl.BlockSpec(memory_space=pltpu.VMEM), pl.BlockSpec(memory_space=pltpu.SMEM)
    message = jax.ShapeDtypeStruct((MAXT * rows + SUBS, LANES), jnp.int16)
    slots = devices * MAXT
    *messages, weight = pl.pallas_call(
        functools.partial(sum_hours_kernel, devices, hours, levels),
        out_shape=[message] * devices + [jax.ShapeDtypeStruct((SUBS, LANES), jnp.float32)],
        in_specs=[smem, hbm, hbm, hbm],
        out_specs=[vmem] * (devices + 1),
        scratch_shapes=[
            pltpu.VMEM((slots, rows, LANES), jnp.int16),
            pltpu.VMEM((slots, SUBS, LANES), jnp.int32),
            pltpu.VMEM(flat.shape, flat.dtype),
            pltpu.SMEM(owners.shape, owners.dtype),
            pltpu.SMEM(thickness.shape, thickness.dtype),
            pltpu.SemaphoreType.DMA((2,)),
            pltpu.SemaphoreType.DMA((tiles,)),
        ],
        compiler_params=pltpu.CompilerParams(vmem_limit_bytes=8 << 20),
    )(lengths, owners, thickness, flat)
    received = [messages[0]]
    for step in send_order(devices):
        pairs = [(source, target(source, step, devices)) for source in range(devices)]
        received.append(lax.ppermute(messages[step], "tm", pairs))
    share = jax.ShapeDtypeStruct((MAXT, rows // levels, LANES), jnp.float32)
    daily, *shares = pl.pallas_call(
        functools.partial(daily_kernel, devices, levels),
        out_shape=[pltpu.VMEM((MAXT, rows, LANES), jnp.float32)] + [share] * levels,
        in_specs=[vmem] * (devices + 1),
        out_specs=[vmem] * (levels + 1),
        scratch_shapes=[pltpu.VMEM((MAXT, rows, LANES), jnp.float32)],
        compiler_params=pltpu.CompilerParams(vmem_limit_bytes=8 << 20),
    )(weight, *received)
    terms = [shares[0]]
    for step in reversed(range(1, levels)):
        if levels & (levels - 1) == 0:
            pairs = [(source, source ^ step) for source in range(levels)]
        else:
            pairs = [(source, (source + step) % levels) for source in range(levels)]
        terms.append(lax.ppermute(shares[step], "lev", pairs))
    column = pl.pallas_call(
        column_kernel,
        out_shape=share,
        in_specs=[vmem] * levels,
        out_specs=vmem,
        compiler_params=pltpu.CompilerParams(vmem_limit_bytes=8 << 20),
    )(*terms)
    return daily.reshape(1, MAXT, 1, cells), column.reshape(MAXT, 1, cells // levels)


def solution(mesh):
    days = mesh.shape["tm"] * HOURS_DEV // 24
    placed = (P("lev", "tm", None, None), P("tm"), P(), P())
    return jax.shard_map(
        one_day if days == 1 else many_days,
        mesh=mesh,
        in_specs=placed,
        out_specs=(P("lev", "tm", None, None), P("tm", None, "lev")),
        check_vma=False,
    )
```
